256 devices in a mesh: row: 16 (over z_lo, y), col: 16 (over x, z_hi, core).
Axes of the slice: x: 4, y: 4, z: 8 (z_hi: 2, z_lo: 4; z = z_hi * 4 + z_lo), core: 2. Of those that a mesh axis runs over, the one named last changes fastest.
Arguments:
- queries: bfloat16 [32768, 1792], P(('row', 'col')), may hold values from -120 to 120, as said below
- keys_values: bfloat16 [32768, 512], P(('row', 'col')), may hold values from -5.5 to 5.5
- segment_ids: int32 [32768], P(('row', 'col')), may hold values from 0 to 7, never falling along the last dimension, each value on 1 to 20480 neighbouring positions
Outputs:
- context: bfloat16 [32768, 1792], P(('row', 'col'))
The draws below stay inside these ranges and needn't reach their ends.
Inputs may be any that keep to these rules, and one draw needn't show every extreme that they name: `queries`: some query rows may be large multiples of a visible key, so scores reach about 270.
All inputs are finite; a program needn't handle non-finite values.
Results may differ from the reference program's by a relative error of at most 0.017.
Values may be sent and summed in bfloat16 or wider, within the bound.
No kernel may reach another device: no remote copies, remote signals or barrier semaphores. Data moves between devices by JAX's collectives and lax.ppermute only.
A program may use at most 128 MiB of HBM per device.

```python
import math
import jax
import jax.numpy as jnp
import numpy as np
from jax import lax

HD = 128
KVH = 2
GROUP = 7
TOK_DEV = 128
SEQ = 32768
DOCS = 8
MAXDOC = 20480
N_ROW = 16
N_COL = 16


def draw_pair(key):
    keys = jnp.clip(jax.random.normal(jax.random.fold_in(key, 102), (SEQ, KVH, HD), jnp.float32), -5.0, 5.0)
    values = jnp.clip(jax.random.normal(jax.random.fold_in(key, 103), (SEQ, KVH, HD), jnp.float32), -5.0, 5.0)
    base = jax.random.normal(jax.random.fold_in(key, 101), (SEQ, KVH, GROUP, HD), jnp.float32)
    queries = 2.5 * jnp.clip(base, -5.0, 5.0)
    return (queries, keys, values)


def draw_queries(key, part):
    queries, keys, values = draw_pair(key)
    return queries.reshape(SEQ, KVH * GROUP * HD).astype(jnp.bfloat16)


def draw_keys_values(key, part):
    queries, keys, values = draw_pair(key)
    joined = jnp.concatenate([keys.reshape(SEQ, KVH * HD), values.reshape(SEQ, KVH * HD)], axis=1)
    return joined.astype(jnp.bfloat16)


def profile(number_of, total, limit, skew):
    weights = [(1 << 20) // math.isqrt(rank ** skew) + 1 for rank in range(2, number_of + 1)]
    spare, given = total - limit - (number_of - 1), [1] * (number_of - 1)
    while spare > 0:
        candidates = [i for i in range(number_of - 1) if given[i] < limit]
        pool, left = sum([weights[i] for i in candidates]), spare
        for i in candidates:
            addition = min(limit - given[i], max(1, left * weights[i] // pool), spare)
            given[i] = given[i] + addition
            spare = spare - addition
    return np.array([limit] + given)


def ragged_sizes(own_key, count, total, limit, skew):
    if count == 2:
        one = jax.random.randint(own_key, (), max(1, total - limit), min(limit, total - 1) + 1)
        return jnp.stack([one, total - one])
    lengths = jnp.asarray(profile(count, total, limit, skew), jnp.int32)
    twos = (count - 1) // 2
    source_of, sink = lengths[1:1 + 2 * twos:2], lengths[2:2 + 2 * twos:2]
    room = jnp.minimum(source_of - 1, limit - sink)
    shifted = jax.random.randint(jax.random.fold_in(own_key, 1), (twos,), 0, 1 << 20) % (room + 1)
    lengths = lengths.at[1:1 + 2 * twos:2].set(source_of - shifted).at[2:2 + 2 * twos:2].set(sink + shifted)
    return lengths[jax.random.permutation(jax.random.fold_in(own_key, 2), count)]


def setup_inputs(seed: int = 0) -> dict:
    splits = jax.random.split(jax.random.key(seed), 4)
    return {
        "queries": draw_queries(jax.random.fold_in(splits[3], 71), 0),
        "keys_values": draw_keys_values(jax.random.fold_in(splits[3], 71), 0),
        "segment_ids": jnp.searchsorted(jnp.cumsum(ragged_sizes(splits[2], DOCS, SEQ, MAXDOC, 0)), jnp.arange(SEQ), side="right").astype(jnp.int32),
    }


NEG = -1e+30

def reference(queries, keys_values, segment_ids):
    seq = queries.shape[0]
    slab = N_COL * TOK_DEV
    pad = MAXDOC
    span = pad + slab
    per_col = span // N_COL
    scale = 1.0 / math.sqrt(HD)
    feat = 2 * KVH * HD
    kv_pad = jnp.concatenate([jnp.zeros((pad, feat), keys_values.dtype), keys_values], axis=0)
    seg_pad = jnp.concatenate([jnp.full((pad,), -1, jnp.int32), segment_ids.astype(jnp.int32)], axis=0)
    pos_pad = jnp.arange(seq + pad, dtype=jnp.int32) - jnp.int32(pad)

    def slab_fn(index):
        start = (index * slab).astype(jnp.int32)
        q_rows = lax.dynamic_slice_in_dim(queries, start, slab, 0).astype(jnp.float32)
        q_rows = q_rows.reshape(slab, KVH, GROUP, HD)
        q_pos = start + jnp.arange(slab, dtype=jnp.int32)
        q_seg = lax.dynamic_slice_in_dim(segment_ids.astype(jnp.int32), start, slab, 0)
        kv_win = lax.dynamic_slice_in_dim(kv_pad, start, span, 0)
        seg_win = lax.dynamic_slice_in_dim(seg_pad, start, span, 0)
        pos_win = lax.dynamic_slice_in_dim(pos_pad, start, span, 0)
        kv_cols = kv_win.reshape(span // slab, N_COL, TOK_DEV, feat).transpose(1, 0, 2, 3).reshape(N_COL, per_col, feat)
        seg_cols = seg_win.reshape(span // slab, N_COL, TOK_DEV).transpose(1, 0, 2).reshape(N_COL, per_col)
        pos_cols = pos_win.reshape(span // slab, N_COL, TOK_DEV).transpose(1, 0, 2).reshape(N_COL, per_col)

        def column_fn(args):
            kv_c, seg_c, pos_c = args
            keys = kv_c[:, :KVH * HD].astype(jnp.float32).reshape(per_col, KVH, HD)
            values = kv_c[:, KVH * HD:].astype(jnp.float32).reshape(per_col, KVH, HD)
            visible = (pos_c[None, :] <= q_pos[:, None]) & (seg_c[None, :] == q_seg[:, None])
            shown = visible[:, None, None, :]
            scores = jnp.einsum('qgrd,kgd->qgrk', q_rows, keys) * scale
            scores = jnp.where(shown, scores, NEG)
            top_c = lax.optimization_barrier(jnp.max(scores, axis=-1))
            weights = jnp.where(shown, jnp.exp(scores - top_c[..., None]), 0.0)
            total_c = lax.optimization_barrier(jnp.sum(weights, axis=-1))
            weight_b = lax.optimization_barrier(weights.astype(jnp.bfloat16)).astype(jnp.float32)
            acc_c = jnp.einsum('qgrk,kgd->qgrd', weight_b, values)
            return (top_c, total_c, acc_c)
        top_c, total_c, acc_c = lax.map(column_fn, (kv_cols, seg_cols, pos_cols))
        top = lax.optimization_barrier(jnp.max(top_c, axis=0))
        factor = jnp.exp(top_c - top[None])
        term = lax.optimization_barrier((acc_c * factor[..., None]).astype(jnp.bfloat16)).astype(jnp.float32)
        mass = lax.optimization_barrier((total_c * factor).astype(jnp.bfloat16)).astype(jnp.float32)
        out = lax.optimization_barrier(jnp.sum(term, axis=0)) / lax.optimization_barrier(jnp.sum(mass, axis=0))[..., None]
        return out.reshape(slab, KVH * GROUP * HD).astype(jnp.bfloat16)
    slabs = lax.map(slab_fn, jnp.arange(N_ROW, dtype=jnp.int32))
    return slabs.reshape(seq, KVH * GROUP * HD)
```

```python
import functools
import math

import jax
import jax.numpy as jnp
from jax import lax
from jax.experimental import pallas as pl
from jax.experimental.pallas import tpu as pltpu
from jax.sharding import PartitionSpec as P

HD = 128
KVH = 2
GROUP = 7
HEADS = KVH * GROUP
TOK = 128
DOCS = 8
ROWS = GROUP * TOK
FEAT = KVH * HD
EXTRA = 8
RUN = 512
SCALE = 1.0 / math.sqrt(HD)
LOG2 = SCALE * math.log2(math.e)
LOW = -1e20
MASKED = -1e30
AXES = ("row", "col")


def digits(b):
    zl, y, x, zh, c = b // 64, b // 16 % 4, b // 4 % 4, b // 2 % 2, b % 2
    return zh * 4 + zl, y, x, c


def block_of(z, y, x, c):
    return z % 4 * 64 + y * 16 + x * 4 + z // 4 * 2 + c


def from_offset(value, dz=0, dy=0, dx=0, dc=0):
    pairs = []
    for b in range(256):
        z, y, x, c = digits(b)
        source = block_of((z + dz) % 8, (y + dy) % 4, (x + dx) % 4, (c + dc) % 2)
        pairs.append((source, b))
    return lax.ppermute(value, AXES, pairs)


def doc_start(meta_ref, pos):
    start = jnp.zeros_like(pos)
    for d in range(1, DOCS):
        here = meta_ref[8 + d]
        start = jnp.maximum(start, jnp.where(here <= pos, here, 0))
    return start


def attend_kernel(meta_ref, q_ref, *refs):
    pieces = refs[:10]
    out_ref, kv_buf, q_buf, top_buf, acc_buf, start_buf, sems = refs[10:]
    z0, y0, x0, c0, q_base = (meta_ref[i] for i in range(5))
    own, other = pieces[:5], pieces[5:]

    def run_base(t):
        zl = (z0 + t % 4) % 4
        y = (y0 + t // 4) % 4
        return zl * 8192 + y * 2048 + x0 * 512

    q_low = doc_start(meta_ref, q_base)
    q_high = doc_start(meta_ref, q_base + TOK - 1)

    def seen(t):
        base = run_base(t)
        return (base <= q_base + TOK - 1) & (base + RUN > q_low)

    for t in range(16):
        dy, w = t // 4, t % 4

        @pl.when(seen(t))
        def _(t=t, dy=dy, w=w):
            for a in range(2):
                for cc in range(2):
                    side = (own, other)[cc]
                    zz = w + 4 * a
                    place = pl.ds((2 * a + cc) * TOK, TOK)
                    rows = pl.ds(0, TOK)
                    if dy == 2:
                        for half, src in ((0, side[3]), (1, side[4])):
                            pltpu.make_async_copy(
                                src.at[zz, rows],
                                kv_buf.at[t, place, pl.ds(half * FEAT, FEAT)],
                                sems.at[t],
                            ).start()
                    else:
                        src = side[{0: 0, 1: 1, 3: 2}[dy]]
                        pltpu.make_async_copy(
                            src.at[zz, rows], kv_buf.at[t, place], sems.at[t]
                        ).start()

    for h in range(HEADS):
        q_buf[h // GROUP, pl.ds(h % GROUP * TOK, TOK), :] = q_ref[:, h * HD : (h + 1) * HD]
    top_buf[...] = jnp.full_like(top_buf, LOW)
    acc_buf[...] = jnp.zeros_like(acc_buf)
    q_pos = q_base + lax.broadcasted_iota(jnp.int32, (TOK, TOK), 0)
    start_buf[...] = doc_start(meta_ref, q_pos)
    ones = jnp.ones((RUN, HD), jnp.bfloat16)

    def update(t, masked):
        if masked:
            base = run_base(t)
            lane = lax.broadcasted_iota(jnp.int32, (TOK, TOK), 1)
            qp = q_base + lax.broadcasted_iota(jnp.int32, (TOK, TOK), 0)
            first = start_buf[...]
            shown = []
            for a in range(2):
                for cc in range(2):
                    zh = (z0 + t % 4 + 4 * a) % 8 // 4
                    c = (c0 + cc) % 2
                    kp = base + (zh * 2 + c) * TOK + lane
                    shown.append((kp <= qp) & (kp >= first))
            shown = jnp.concatenate(shown, axis=1)
        for g in range(KVH):
            k = kv_buf[t, :, g * HD : (g + 1) * HD]
            v = kv_buf[t, :, FEAT + g * HD : FEAT + (g + 1) * HD]
            s = lax.dot_general(
                q_buf[g], k, (((1,), (1,)), ((), ())), preferred_element_type=jnp.float32
            )
            if masked:
                s = jnp.where(shown[None], s.reshape(GROUP, TOK, RUN), MASKED).reshape(ROWS, RUN)
            old = top_buf[g]
            top = jnp.maximum(old, jnp.max(s, axis=-1, keepdims=True))
            p = jnp.exp2((s - jnp.concatenate([top] * 4, axis=1)) * LOG2).astype(jnp.bfloat16)
            factor = jnp.exp2((old - top) * LOG2)
            more = jnp.dot(
                p, jnp.concatenate([v, ones], axis=1), preferred_element_type=jnp.float32
            )
            acc_buf[g] = acc_buf[g] * jnp.concatenate([factor] * 2, axis=1) + more
            top_buf[g] = top

    def step(t, carry):
        base = run_base(t)
        whole = (base + RUN - 1 <= q_base) & (base >= q_high)
        visible = seen(t)

        @pl.when(visible)
        def _():
            pltpu.make_async_copy(kv_buf.at[t], kv_buf.at[t], sems.at[t]).wait()

        @pl.when(visible & whole)
        def _():
            update(t, False)

        @pl.when(visible & jnp.logical_not(whole))
        def _():
            update(t, True)

        return carry

    lax.fori_loop(0, 16, step, 0)

    lane = lax.broadcasted_iota(jnp.int32, (TOK, HD), 1)
    stat = jnp.zeros((TOK, HD), jnp.float32)
    for h in range(HEADS):
        g, rows = h // GROUP, pl.ds(h % GROUP * TOK, TOK)
        total = acc_buf[g, rows, HD:]
        some = total > 0
        safe = jnp.where(some, total, 1.0)
        out_ref[:, h * HD : (h + 1) * HD] = (acc_buf[g, rows, :HD] / safe).astype(jnp.bfloat16)
        level = jnp.where(some, top_buf[g, rows, :] * SCALE + jnp.log(safe), MASKED)
        high = level.astype(jnp.bfloat16).astype(jnp.float32)
        rest = level - high
        middle = rest.astype(jnp.bfloat16).astype(jnp.float32)
        stat = jnp.where(lane == h, high, stat)
        stat = jnp.where(lane == 16 + h, middle, stat)
        stat = jnp.where(lane == 32 + h, rest - middle, stat)
    out_ref[:, HEADS * HD :] = stat.astype(jnp.bfloat16)


def attend(meta, q, pieces):
    any_spec = pl.BlockSpec(memory_space=pl.ANY)
    return pl.pallas_call(
        attend_kernel,
        out_shape=jax.ShapeDtypeStruct((TOK, (HEADS + 1) * HD), jnp.bfloat16),
        in_specs=[pl.BlockSpec(memory_space=pltpu.SMEM), pl.BlockSpec(memory_space=pltpu.VMEM)]
        + [any_spec] * len(pieces),
        out_specs=pl.BlockSpec(memory_space=pltpu.VMEM),
        scratch_shapes=[
            pltpu.VMEM((16, RUN, 2 * FEAT), jnp.bfloat16),
            pltpu.VMEM((KVH, ROWS, HD), jnp.bfloat16),
            pltpu.VMEM((KVH, ROWS, HD), jnp.float32),
            pltpu.VMEM((KVH, ROWS, 2 * HD), jnp.float32),
            pltpu.VMEM((TOK, TOK), jnp.int32),
            pltpu.SemaphoreType.DMA((16,)),
        ],
        name="attend",
    )(meta, q, *pieces)


def combine_kernel(*refs):
    parts, out_ref = refs[:-1], refs[-1]
    stats = [part[:, HEADS * HD :].astype(jnp.float32) for part in parts]
    for h in range(HEADS):
        levels = [
            s[:, h : h + 1] + s[:, 16 + h : 17 + h] + s[:, 32 + h : 33 + h] for s in stats
        ]
        best = functools.reduce(jnp.maximum, levels)
        weights = [jnp.exp(level - best) for level in levels]
        total = functools.reduce(jnp.add, weights)
        value = functools.reduce(
            jnp.add,
            [
                part[:, h * HD : (h + 1) * HD].astype(jnp.float32) * w
                for part, w in zip(parts, weights)
            ],
        )
        out_ref[:, h * HD : (h + 1) * HD] = (value / total).astype(jnp.bfloat16)


def combine(parts):
    return pl.pallas_call(
        combine_kernel,
        out_shape=jax.ShapeDtypeStruct((TOK, HEADS * HD), jnp.bfloat16),
        name="combine",
    )(*parts)


def gather_column(message):
    ups, downs = [message], [message]
    for step in range(4):
        ups.append(from_offset(ups[-1], dz=1))
        if step < 3:
            downs.append(from_offset(downs[-1], dz=-1))
    here = jnp.stack(ups + downs[:0:-1])
    above = from_offset(here, dy=1)
    below = from_offset(here, dy=-1)
    far_k = from_offset(above[:, :, :FEAT], dy=1)
    far_v = from_offset(below[:, :, FEAT:], dy=-1)
    own = [here, above, below, far_k, far_v]
    return own + [from_offset(piece, dc=1) for piece in own]


def shards(queries, keys_values, segment_ids):
    b = lax.axis_index("row") * 16 + lax.axis_index("col")
    z, y, x, c = digits(b)
    docs = jnp.arange(DOCS, dtype=jnp.int32)
    counts = jnp.sum(segment_ids[None, :] < docs[:, None], axis=1)
    extra = jnp.pad(counts.astype(jnp.bfloat16)[None], ((0, EXTRA - 1), (0, 2 * FEAT - DOCS)))
    pieces = gather_column(jnp.concatenate([keys_values, extra], axis=0))
    column = sum(
        jnp.sum(p[:, TOK, :DOCS].astype(jnp.float32), axis=0) for i, p in enumerate(pieces) if i % 5 != 4
    )
    column = jnp.broadcast_to(column[None], (8, DOCS))
    column = column + from_offset(column, dx=1)
    column = column + from_offset(column, dx=2)
    starts = column[0].astype(jnp.int32)

    queries, _ = lax.optimization_barrier((queries, pieces[0][0, 0, 0]))
    outs = []
    for j in (2, 1, -1, 0):
        q = from_offset(queries, dz=j, dx=j) if j else queries
        source = block_of((z + j) % 8, y, (x + j) % 4, c)
        meta = jnp.concatenate(
            [jnp.stack([z, y, x, c, source * TOK, z, z, z]).astype(jnp.int32), starts]
        )
        out = attend(meta, q, pieces)
        outs.append(from_offset(out, dz=-j, dx=-j) if j else out)
    return combine(outs)


def solution(mesh):
    in_specs = (P(AXES, None), P(AXES, None), P(AXES))
    return jax.shard_map(
        shards, mesh=mesh, in_specs=in_specs, out_specs=P(AXES, None), check_vma=False
    )
```
